32 devices in a mesh: ctx: 8 (over z, y), head: 4 (over x, core).
Axes of the slice: x: 2, y: 2, z: 4, core: 2. Of those that a mesh axis runs over, the one named last changes fastest.
Arguments:
- queries: bfloat16 [8192, 1024], P('ctx', 'head'), parts along dimension 1, may hold values from -15 to 15
- key_rows: bfloat16 [8192, 512], P('ctx', 'head'), parts along dimension 1, may hold values from -6 to 6
- value_rows: bfloat16 [8192, 512], P('ctx', 'head'), parts along dimension 1, may hold values from -16 to 16
- block_order: int32 [8], replicated, may hold values from 0 to 7, each once
Outputs:
- attended: bfloat16 [8192, 1024], P('ctx', 'head'), parts along dimension 1
The draws below stay inside these ranges and needn't reach their ends.
There are 4 independent parts, one for each index of `head`. The reference program is written for one: setup_inputs(seed, part) draws one part's arguments, and reference() takes and returns one part's arrays. A program takes and returns all parts, laid end to end along the dimension named above; an argument that names none is the same for every part. Nothing has to cross between parts.
Inputs may be any that keep to these rules, and one draw needn't show every extreme that they name: `block_order`: each block number appears once.
All inputs are finite; a program needn't handle non-finite values.
Results may differ from the reference program's by a relative error of at most 0.0033.
Values may be sent and summed in bfloat16 or wider, within the bound.
A program may use at most 128 MiB of HBM per device.

```python
import jax
import jax.numpy as jnp
from jax import lax

HD = 128
QH = 2
TOK_DEV = 1024
BLOCKS = 8
SEQ = 8192


def paired_rows(key):
    folded = jax.random.fold_in(key, 2711)
    query_key, row_key = jax.random.split(folded, 2)
    queries = jnp.clip(2.5 * jax.random.normal(query_key, (SEQ, QH * HD), jnp.float32), -15.0, 15.0)
    key_rows = jnp.clip(jax.random.normal(row_key, (SEQ, HD), jnp.float32), -6.0, 6.0)
    return (queries, key_rows)


def draw_queries(key, part):
    return paired_rows(key)[0].astype(jnp.bfloat16)


def draw_key_rows(key, part):
    return paired_rows(key)[1].astype(jnp.bfloat16)


def block_levels(rng, dims, cuts, low, top_value):
    level = 1.0
    for position, blocks in cuts:
        heights = jax.random.uniform(jax.random.fold_in(jax.random.fold_in(rng, 6), position), (blocks,), jnp.float32, low / len(cuts), top_value / len(cuts))
        level = level * jnp.repeat(jnp.exp(heights), dims[position] // blocks).reshape((-1,) + (1,) * (len(dims) - 1 - position))
    return level


def bell_draw(own_key, dims, deviation, bound, cuts=(), kind=jnp.bfloat16):
    level = block_levels(own_key, dims, cuts, -0.22, 0.18) if cuts else 1.0
    entries = jax.random.normal(own_key, dims, jnp.float32) * deviation * level
    return jnp.minimum(jnp.maximum(entries, -bound), bound).astype(kind)


def setup_inputs(seed: int = 0, part: int = 0) -> dict:
    key_list = jax.random.split(jax.random.key(seed), 5)
    part_splits = jax.random.split(jax.random.fold_in(key_list[4], part), 5)
    queries = draw_queries(jax.random.fold_in(jax.random.fold_in(key_list[4], part), 71), part)
    key_rows = draw_key_rows(jax.random.fold_in(jax.random.fold_in(key_list[4], part), 71), part)
    value_rows = bell_draw(part_splits[2], (SEQ, HD), 4.0, 16.0, ((0, 8),))
    block_order = jax.random.permutation(key_list[3], BLOCKS).astype(jnp.int32)
    return dict(queries=queries, key_rows=key_rows, value_rows=value_rows, block_order=block_order)


score_scale = 168.0 ** -0.5


def positions_of(block_order, count):
    row_ids = jnp.arange(count, dtype=jnp.int32)
    return block_order[row_ids // TOK_DEV] * TOK_DEV + row_ids % TOK_DEV


def reference(queries, key_rows, value_rows, block_order):
    key_pos = positions_of(block_order, SEQ)
    keys_wide = key_rows.astype(jnp.float32)
    values_wide = value_rows.astype(jnp.float32)

    def one_block(block_index):
        row_start = block_index * TOK_DEV
        query_block = lax.dynamic_slice_in_dim(queries, row_start, TOK_DEV, 0)
        query_block = query_block.astype(jnp.float32).reshape(TOK_DEV, QH, HD)
        query_pos = lax.dynamic_slice_in_dim(key_pos, row_start, TOK_DEV, 0)

        def key_step(carry, key_index):
            run_sum, run_max, run_total = carry
            key_start = key_index * TOK_DEV
            tile_keys = lax.dynamic_slice_in_dim(keys_wide, key_start, TOK_DEV, 0)
            tile_values = lax.dynamic_slice_in_dim(values_wide, key_start, TOK_DEV, 0)
            tile_pos = lax.dynamic_slice_in_dim(key_pos, key_start, TOK_DEV, 0)
            scores = jnp.einsum("qhd,kd->hqk", query_block, tile_keys) * score_scale
            visible = tile_pos[None, :] <= query_pos[:, None]
            scores = jnp.where(visible[None], scores, -jnp.inf)
            block_max = jnp.maximum(jnp.max(scores, axis=2), -1e30)
            weights = jnp.exp(scores - block_max[:, :, None])
            block_total = jnp.sum(weights, axis=2)
            rounded = lax.optimization_barrier(weights.astype(jnp.bfloat16)).astype(jnp.float32)
            block_sum = jnp.einsum("hqk,kd->hqd", rounded, tile_values)
            new_max = jnp.maximum(run_max, block_max)
            scale_old = jnp.exp(run_max - new_max)
            scale_new = jnp.exp(block_max - new_max)
            run_sum = run_sum * scale_old[:, :, None] + block_sum * scale_new[:, :, None]
            run_total = run_total * scale_old + block_total * scale_new
            return (run_sum, new_max, run_total), None

        start = (jnp.zeros((QH, TOK_DEV, HD), jnp.float32),
                 jnp.full((QH, TOK_DEV), -1e30, jnp.float32),
                 jnp.zeros((QH, TOK_DEV), jnp.float32))
        final, unused = lax.scan(key_step, start, jnp.arange(BLOCKS, dtype=jnp.int32))
        blended = final[0] / final[2][:, :, None]
        return blended.transpose(1, 0, 2).reshape(TOK_DEV, QH * HD).astype(jnp.bfloat16)

    outputs = lax.map(one_block, jnp.arange(BLOCKS, dtype=jnp.int32))
    return outputs.reshape(SEQ, QH * HD)
```

```python
import functools

import jax
import jax.numpy as jnp
from jax import lax
from jax.experimental import pallas as pl
from jax.experimental.pallas import tpu as pltpu
from jax.sharding import PartitionSpec as P

HD = 128
QH = 2
CHUNKS = 4
TILE = 256
SCALE2 = 168.0 ** (-0.5) * 1.4426950408889634
LOW = -1e30


def ring_place(index, count):
    side = lax.rem(index, 2)
    level = lax.div(index, 2)
    return level * (1 - side) + (count - 1 - level) * side


def ring_index(place, count):
    side = lax.div(place, count // 2)
    level = place * (1 - side) + (count - 1 - place) * side
    return level * 2 + side


def lanes(column, width):
    return jnp.concatenate([column] * (width // HD), axis=1)


def dot_t(a, b):
    return lax.dot_general(a, b, (((1,), (1,)), ((), ())), preferred_element_type=jnp.float32)


def lane_sum(weights):
    total = weights[:, :HD]
    for start in range(HD, weights.shape[1], HD):
        total = total + weights[:, start : start + HD]
    return total


def kernel(
    count, order_ref, q_ref, k_ref, v_ref, out_ref,
    left_k, left_v, right_k, right_v, acc, peak, total,
    to_right, to_left, from_left, from_right,
):
    me = lax.axis_index("ctx")
    rows = q_ref.shape[0]
    piece = rows // CHUNKS
    steps = CHUNKS * (count - 1) // 2
    place = ring_place(me, count)
    right = ring_index(lax.rem(place + 1, count), count)
    left = ring_index(lax.rem(place + count - 1, count), count)

    barrier = pltpu.get_barrier_semaphore()
    for neighbour in (left, right):
        pl.semaphore_signal(barrier, inc=1, device_id={"ctx": neighbour}, device_id_type=pl.DeviceIdType.MESH)
    pl.semaphore_wait(barrier, 2)

    def copies(j, to_the_right, k_src, v_src):
        k_dst, v_dst = (left_k, left_v) if to_the_right else (right_k, right_v)
        send, recv = (to_right, from_left) if to_the_right else (to_left, from_right)
        target = right if to_the_right else left
        return [
            pltpu.make_async_remote_copy(
                src_ref=src, dst_ref=dst.at[j], send_sem=send.at[j, which], recv_sem=recv.at[j, which],
                device_id={"ctx": target}, device_id_type=pl.DeviceIdType.MESH,
            )
            for which, (src, dst) in enumerate(((k_src, k_dst), (v_src, v_dst)))
        ]

    def own(j, to_the_right):
        at = (j if to_the_right else (j + CHUNKS // 2) % CHUNKS) * piece
        return k_ref.at[pl.ds(at, piece)], v_ref.at[pl.ds(at, piece)]

    for j in range(CHUNKS):
        for way in (True, False):
            for copy in copies(j, way, *own(j, way)):
                copy.start()

    for head in range(QH):
        cols = slice(head * HD, (head + 1) * HD)
        for tile in range(rows // TILE):
            here = slice(tile * TILE, (tile + 1) * TILE)
            width = (tile + 1) * TILE
            scores = dot_t(q_ref[here, cols], k_ref[:width, :])
            row_ids = lax.broadcasted_iota(jnp.int32, (TILE, width), 0) + tile * TILE
            column_ids = lax.broadcasted_iota(jnp.int32, (TILE, width), 1)
            scores = jnp.where(column_ids <= row_ids, scores, LOW)
            top = jnp.broadcast_to(jnp.max(scores, axis=1, keepdims=True), (TILE, HD))
            weights = jnp.exp2((scores - lanes(top, width)) * SCALE2)
            total[head, here, :] = lane_sum(weights)
            acc[head, here, :] = jnp.dot(
                weights.astype(jnp.bfloat16), v_ref[:width, :], preferred_element_type=jnp.float32
            )
            peak[head, here, :] = top

    mine = order_ref[me]

    def absorb(j, carry):
        for way in (True, False):
            for copy in copies(j, way, *own(0, way)):
                copy.wait_recv()

        @pl.when(j + CHUNKS < steps)
        def _():
            for way, k_src, v_src in ((True, left_k, left_v), (False, right_k, right_v)):
                for copy in copies(j + CHUNKS, way, k_src.at[j], v_src.at[j]):
                    copy.start()

        far = 1 + lax.div(j, CHUNKS)
        see_left = order_ref[ring_index(lax.rem(place + count - far, count), count)] < mine
        see_right = order_ref[ring_index(lax.rem(place + far, count), count)] < mine

        def tile_step(tile, carry):
            here = pl.ds(pl.multiple_of(tile * TILE, TILE), TILE)
            for head in range(QH):
                cols = slice(head * HD, (head + 1) * HD)
                q = q_ref[here, cols]
                first = dot_t(q, left_k[j])
                second = dot_t(q, right_k[j])
                old = peak[head, here, :]
                top_first = jnp.where(see_left, jnp.max(first, axis=1, keepdims=True), LOW)
                top_second = jnp.where(see_right, jnp.max(second, axis=1, keepdims=True), LOW)
                top = jnp.maximum(old, jnp.maximum(top_first, top_second))
                keep = jnp.exp2((old - top) * SCALE2)
                shift_first = jnp.where(see_left, top, -LOW)
                shift_second = jnp.where(see_right, top, -LOW)
                w_first = jnp.exp2((first - lanes(shift_first, piece)) * SCALE2)
                w_second = jnp.exp2((second - lanes(shift_second, piece)) * SCALE2)
                peak[head, here, :] = top
                total[head, here, :] = total[head, here, :] * keep + (lane_sum(w_first) + lane_sum(w_second))
                acc[head, here, :] = acc[head, here, :] * keep + (
                    jnp.dot(w_first.astype(jnp.bfloat16), left_v[j], preferred_element_type=jnp.float32)
                    + jnp.dot(w_second.astype(jnp.bfloat16), right_v[j], preferred_element_type=jnp.float32)
                )
            return carry

        return lax.fori_loop(0, rows // TILE, tile_step, carry)

    lax.fori_loop(0, steps, absorb, 0)

    for head in range(QH):
        cols = slice(head * HD, (head + 1) * HD)
        whole = jnp.sum(total[head], axis=1, keepdims=True)
        out_ref[:, cols] = (acc[head] / whole).astype(out_ref.dtype)

    def drain(j, carry):
        for way in (True, False):
            for copy in copies(j, way, *own(0, way)):
                copy.wait_send()
        return carry

    lax.fori_loop(0, steps, drain, 0)


def solution(mesh):
    count = mesh.shape["ctx"]
    steps = CHUNKS * (count - 1) // 2

    def body(queries, key_rows, value_rows, block_order):
        rows = queries.shape[0]
        piece = rows // CHUNKS
        slots = pltpu.VMEM((steps, piece, HD), jnp.bfloat16)
        stats = pltpu.VMEM((QH, rows, HD), jnp.float32)
        sems = pltpu.SemaphoreType.DMA((steps, 2))
        vmem = pl.BlockSpec(memory_space=pltpu.VMEM)
        return pl.pallas_call(
            functools.partial(kernel, count),
            out_shape=jax.ShapeDtypeStruct(queries.shape, queries.dtype),
            in_specs=[pl.BlockSpec(memory_space=pltpu.SMEM), vmem, vmem, vmem],
            out_specs=vmem,
            scratch_shapes=[slots] * 4 + [stats] * 3 + [sems] * 4,
            compiler_params=pltpu.CompilerParams(
                collective_id=0, has_side_effects=True, vmem_limit_bytes=48 * 1024 * 1024
            ),
        )(block_order, queries, key_rows, value_rows)

    in_specs = (P("ctx", "head"), P("ctx", "head"), P("ctx", "head"), P())
    return jax.shard_map(body, mesh=mesh, in_specs=in_specs, out_specs=P("ctx", "head"), check_vma=False)
```

```python
import functools

import jax
import jax.numpy as jnp
from jax import lax
from jax.experimental import pallas as pl
from jax.experimental.pallas import tpu as pltpu
from jax.sharding import PartitionSpec as P

HD = 128
QH = 2
CHUNKS = 4
TILE = 1024
EDGE = 256
SCALE2 = 168.0 ** (-0.5) * 1.4426950408889634
LOW = -1e30


def ring_place(index, count):
    side = lax.rem(index, 2)
    level = lax.div(index, 2)
    return level * (1 - side) + (count - 1 - level) * side


def ring_index(place, count):
    side = lax.div(place, count // 2)
    level = place * (1 - side) + (count - 1 - place) * side
    return level * 2 + side


def lanes(column, width):
    return jnp.concatenate([column] * (width // HD), axis=1)


def dot_t(a, b):
    return lax.dot_general(a, b, (((1,), (1,)), ((), ())), preferred_element_type=jnp.float32)


def lane_sum(weights):
    total = weights[:, :HD]
    for start in range(HD, weights.shape[1], HD):
        total = total + weights[:, start : start + HD]
    return total


def kernel(
    count, order_hbm, q_hbm, k_hbm, v_hbm, out_ref,
    order_ref, q_ref, k_ref, v_ref,
    left_k, left_v, right_k, right_v, acc, peak, total,
    to_right, to_left, from_left, from_right, loaded,
):
    me = lax.axis_index("ctx")
    rows = q_ref.shape[0]
    band = min(TILE, rows)
    piece = rows // CHUNKS
    steps = CHUNKS * (count - 1) // 2
    place = ring_place(me, count)
    right = ring_index(lax.rem(place + 1, count), count)
    left = ring_index(lax.rem(place + count - 1, count), count)

    barrier = pltpu.get_barrier_semaphore()
    for neighbour in (left, right):
        pl.semaphore_signal(barrier, inc=1, device_id={"ctx": neighbour}, device_id_type=pl.DeviceIdType.MESH)
    loads = [
        pltpu.make_async_copy(src, dst, loaded.at[which])
        for which, (src, dst) in enumerate(((order_hbm, order_ref), (k_hbm, k_ref), (q_hbm, q_ref), (v_hbm, v_ref)))
    ]
    for load in loads:
        load.start()
    pl.semaphore_wait(barrier, 2)

    def copies(j, to_the_right, k_src, v_src):
        k_dst, v_dst = (left_k, left_v) if to_the_right else (right_k, right_v)
        send, recv = (to_right, from_left) if to_the_right else (to_left, from_right)
        target = right if to_the_right else left
        return [
            pltpu.make_async_remote_copy(
                src_ref=src, dst_ref=dst.at[j], send_sem=send.at[j, which], recv_sem=recv.at[j, which],
                device_id={"ctx": target}, device_id_type=pl.DeviceIdType.MESH,
            )
            for which, (src, dst) in enumerate(((k_src, k_dst), (v_src, v_dst)))
        ]

    def own(j, to_the_right):
        at = (j if to_the_right else (j + CHUNKS // 2) % CHUNKS) * piece
        return k_hbm.at[pl.ds(at, piece)], v_hbm.at[pl.ds(at, piece)]

    for j in range(CHUNKS):
        for way in (True, False):
            for copy in copies(j, way, *own(j, way)):
                copy.start()

    for load in loads:
        load.wait()

    for head in range(QH):
        cols = slice(head * HD, (head + 1) * HD)
        for tile in range(rows // EDGE):
            here = slice(tile * EDGE, (tile + 1) * EDGE)
            width = (tile + 1) * EDGE
            scores = dot_t(q_ref[here, cols], k_ref[:width, :])
            row_ids = lax.broadcasted_iota(jnp.int32, (EDGE, width), 0) + tile * EDGE
            column_ids = lax.broadcasted_iota(jnp.int32, (EDGE, width), 1)
            scores = jnp.where(column_ids <= row_ids, scores, LOW)
            top = jnp.broadcast_to(jnp.max(scores, axis=1, keepdims=True), (EDGE, HD))
            weights = jnp.exp2((scores - lanes(top, width)) * SCALE2)
            total[head, here, :] = lane_sum(weights)
            acc[head, here, :] = jnp.dot(
                weights.astype(jnp.bfloat16), v_ref[:width, :], preferred_element_type=jnp.float32
            )
            peak[head, here, :] = top

    mine = order_ref[me]

    def absorb(j, carry):
        for way in (True, False):
            for copy in copies(j, way, *own(0, way)):
                copy.wait_recv()

        @pl.when(j + CHUNKS < steps)
        def _():
            for way, k_src, v_src in ((True, left_k, left_v), (False, right_k, right_v)):
                for copy in copies(j + CHUNKS, way, k_src.at[j], v_src.at[j]):
                    copy.start()

        far = 1 + lax.div(j, CHUNKS)
        see_left = order_ref[ring_index(lax.rem(place + count - far, count), count)] < mine
        see_right = order_ref[ring_index(lax.rem(place + far, count), count)] < mine

        def tile_step(tile, carry):
            here = pl.ds(pl.multiple_of(tile * band, band), band)
            for head in range(QH):
                cols = slice(head * HD, (head + 1) * HD)
                q = q_ref[here, cols]
                first = dot_t(q, left_k[j])
                second = dot_t(q, right_k[j])
                old = peak[head, here, :]
                top_first = jnp.where(see_left, jnp.max(first, axis=1, keepdims=True), LOW)
                top_second = jnp.where(see_right, jnp.max(second, axis=1, keepdims=True), LOW)
                top = jnp.maximum(old, jnp.maximum(top_first, top_second))
                keep = jnp.exp2((old - top) * SCALE2)
                shift_first = jnp.where(see_left, top, -LOW)
                shift_second = jnp.where(see_right, top, -LOW)
                w_first = jnp.exp2((first - lanes(shift_first, piece)) * SCALE2)
                w_second = jnp.exp2((second - lanes(shift_second, piece)) * SCALE2)
                peak[head, here, :] = top
                total[head, here, :] = total[head, here, :] * keep + (lane_sum(w_first) + lane_sum(w_second))
                acc[head, here, :] = acc[head, here, :] * keep + (
                    jnp.dot(w_first.astype(jnp.bfloat16), left_v[j], preferred_element_type=jnp.float32)
                    + jnp.dot(w_second.astype(jnp.bfloat16), right_v[j], preferred_element_type=jnp.float32)
                )
            return carry

        return lax.fori_loop(0, rows // band, tile_step, carry)

    lax.fori_loop(0, steps, absorb, 0)

    for head in range(QH):
        cols = slice(head * HD, (head + 1) * HD)
        scale = 1.0 / jnp.sum(total[head], axis=1, keepdims=True)
        out_ref[:, cols] = (acc[head] * scale).astype(out_ref.dtype)

    def drain(j, carry):
        for way in (True, False):
            for copy in copies(j, way, *own(0, way)):
                copy.wait_send()
        return carry

    lax.fori_loop(0, steps, drain, 0)


def solution(mesh):
    count = mesh.shape["ctx"]
    steps = CHUNKS * (count - 1) // 2

    def body(queries, key_rows, value_rows, block_order):
        rows = queries.shape[0]
        piece = rows // CHUNKS
        slots = pltpu.VMEM((steps, piece, HD), jnp.bfloat16)
        stats = pltpu.VMEM((QH, rows, HD), jnp.float32)
        sems = pltpu.SemaphoreType.DMA((steps, 2))
        local = [pltpu.SMEM(block_order.shape, block_order.dtype)] + [
            pltpu.VMEM(array.shape, array.dtype) for array in (queries, key_rows, value_rows)
        ]
        return pl.pallas_call(
            functools.partial(kernel, count),
            out_shape=jax.ShapeDtypeStruct(queries.shape, queries.dtype),
            in_specs=[pl.BlockSpec(memory_space=pltpu.HBM)] * 4,
            out_specs=pl.BlockSpec(memory_space=pltpu.VMEM),
            scratch_shapes=local + [slots] * 4 + [stats] * 3 + [sems] * 4 + [pltpu.SemaphoreType.DMA((4,))],
            compiler_params=pltpu.CompilerParams(
                collective_id=0, has_side_effects=True, vmem_limit_bytes=48 * 1024 * 1024
            ),
        )(block_order, queries, key_rows, value_rows)

    in_specs = (P("ctx", "head"), P("ctx", "head"), P("ctx", "head"), P())
    return jax.shard_map(body, mesh=mesh, in_specs=in_specs, out_specs=P("ctx", "head"), check_vma=False)
```

```python
import functools

import jax
import jax.numpy as jnp
from jax import lax
from jax.experimental import pallas as pl
from jax.experimental.pallas import tpu as pltpu
from jax.sharding import PartitionSpec as P

HD = 128
QH = 2
CHUNKS = 4
TILE = 1024
SCALE2 = 168.0 ** (-0.5) * 1.4426950408889634
LOW = -1e30


def ring_place(index, count):
    side = lax.rem(index, 2)
    level = lax.div(index, 2)
    return level * (1 - side) + (count - 1 - level) * side


def ring_index(place, count):
    side = lax.div(place, count // 2)
    level = place * (1 - side) + (count - 1 - place) * side
    return level * 2 + side


def lanes(column, width):
    return jnp.concatenate([column] * (width // HD), axis=1)


def dot_t(a, b):
    return lax.dot_general(a, b, (((1,), (1,)), ((), ())), preferred_element_type=jnp.float32)


def lane_sum(weights):
    total = weights[:, :HD]
    for start in range(HD, weights.shape[1], HD):
        total = total + weights[:, start : start + HD]
    return total


def kernel(
    count, order_hbm, q_hbm, k_hbm, v_hbm, out_ref,
    order_ref, q_ref, kv_ref, from_left, from_right, acc, peak, total,
    to_right_sem, to_left_sem, from_left_sem, from_right_sem, loaded,
):
    me = lax.axis_index("ctx")
    rows = q_ref.shape[0]
    band = min(TILE, rows)
    piece = rows // CHUNKS
    steps = CHUNKS * (count - 1) // 2
    place = ring_place(me, count)
    right = ring_index(lax.rem(place + 1, count), count)
    left = ring_index(lax.rem(place + count - 1, count), count)

    barrier = pltpu.get_barrier_semaphore()
    for neighbour in (left, right):
        pl.semaphore_signal(barrier, inc=1, device_id={"ctx": neighbour}, device_id_type=pl.DeviceIdType.MESH)
    def chunked(src, which):
        return [(src.at[pl.ds(c * piece, piece)], kv_ref.at[c, which]) for c in range(CHUNKS)]

    loads = [
        pltpu.make_async_copy(src, dst, loaded.at[which])
        for which, (src, dst) in enumerate(
            chunked(k_hbm, 0) + chunked(v_hbm, 1) + [(q_hbm, q_ref), (order_hbm, order_ref)]
        )
    ]
    for load in loads:
        load.start()
    for load in loads[:-2]:
        load.wait()
    pl.semaphore_wait(barrier, 2)

    def copy(j, rightward, src, slot):
        dst, send, recv, target = (
            (from_left, to_right_sem, from_left_sem, right)
            if rightward
            else (from_right, to_left_sem, from_right_sem, left)
        )
        return pltpu.make_async_remote_copy(
            src_ref=src.at[slot], dst_ref=dst.at[j], send_sem=send.at[j], recv_sem=recv.at[j],
            device_id={"ctx": target}, device_id_type=pl.DeviceIdType.MESH,
        )

    for j in range(CHUNKS):
        copy(j, True, kv_ref, j).start()
        copy(j, False, kv_ref, (j + CHUNKS // 2) % CHUNKS).start()
    for load in loads[-2:]:
        load.wait()

    for head in range(QH):
        cols = slice(head * HD, (head + 1) * HD)
        for tile in range(CHUNKS):
            here = slice(tile * piece, (tile + 1) * piece)
            width = (tile + 1) * piece
            scores = dot_t(q_ref[here, cols], kv_ref[: tile + 1, 0].reshape(width, HD))
            row_ids = lax.broadcasted_iota(jnp.int32, (piece, width), 0) + tile * piece
            column_ids = lax.broadcasted_iota(jnp.int32, (piece, width), 1)
            scores = jnp.where(column_ids <= row_ids, scores, LOW)
            top = jnp.broadcast_to(jnp.max(scores, axis=1, keepdims=True), (piece, HD))
            weights = jnp.exp2((scores - lanes(top, width)) * SCALE2)
            total[head, here, :] = lane_sum(weights)
            acc[head, here, :] = jnp.dot(
                weights.astype(jnp.bfloat16), kv_ref[: tile + 1, 1].reshape(width, HD), preferred_element_type=jnp.float32
            )
            peak[head, here, :] = top

    mine = order_ref[me]

    def arrive(j):
        copy(j, True, kv_ref, 0).wait_recv()
        copy(j, False, kv_ref, 0).wait_recv()

    def absorb(j, last):
        far = 1 + lax.div(j, CHUNKS)
        see_left = order_ref[ring_index(lax.rem(place + count - far, count), count)] < mine
        see_right = order_ref[ring_index(lax.rem(place + far, count), count)] < mine

        def tile_step(tile, carry):
            here = pl.ds(pl.multiple_of(tile * band, band), band)
            for head in range(QH):
                cols = slice(head * HD, (head + 1) * HD)
                q = q_ref[here, cols]
                first = dot_t(q, from_left[j, 0])
                second = dot_t(q, from_right[j, 0])
                old = peak[head, here, :]
                top_first = jnp.where(see_left, jnp.max(first, axis=1, keepdims=True), LOW)
                top_second = jnp.where(see_right, jnp.max(second, axis=1, keepdims=True), LOW)
                top = jnp.maximum(old, jnp.maximum(top_first, top_second))
                keep = jnp.exp2((old - top) * SCALE2)
                shift_first = jnp.where(see_left, top, -LOW)
                shift_second = jnp.where(see_right, top, -LOW)
                w_first = jnp.exp2((first - lanes(shift_first, piece)) * SCALE2)
                w_second = jnp.exp2((second - lanes(shift_second, piece)) * SCALE2)
                new_total = total[head, here, :] * keep + (lane_sum(w_first) + lane_sum(w_second))
                new_acc = acc[head, here, :] * keep + (
                    jnp.dot(w_first.astype(jnp.bfloat16), from_left[j, 1], preferred_element_type=jnp.float32)
                    + jnp.dot(w_second.astype(jnp.bfloat16), from_right[j, 1], preferred_element_type=jnp.float32)
                )
                if last:
                    inverse = 1.0 / jnp.sum(new_total, axis=1, keepdims=True)
                    out_ref[here, cols] = (new_acc * inverse).astype(out_ref.dtype)
                else:
                    peak[head, here, :] = top
                    total[head, here, :] = new_total
                    acc[head, here, :] = new_acc
            return carry

        lax.fori_loop(0, rows // band, tile_step, 0)

    def advance(j, carry):
        arrive(j)

        @pl.when(j + CHUNKS < steps)
        def _():
            copy(j + CHUNKS, True, from_left, j).start()
            copy(j + CHUNKS, False, from_right, j).start()

        absorb(j, False)
        return carry

    lax.fori_loop(0, steps - 1, advance, 0)
    arrive(steps - 1)
    absorb(steps - 1, True)

    def drain(j, carry):
        copy(j, True, kv_ref, 0).wait_send()
        copy(j, False, kv_ref, 0).wait_send()
        return carry

    lax.fori_loop(0, steps, drain, 0)


def solution(mesh):
    count = mesh.shape["ctx"]
    steps = CHUNKS * (count - 1) // 2

    def body(queries, key_rows, value_rows, block_order):
        rows = queries.shape[0]
        piece = rows // CHUNKS
        slots = pltpu.VMEM((steps, 2, piece, HD), jnp.bfloat16)
        stats = pltpu.VMEM((QH, rows, HD), jnp.float32)
        sems = pltpu.SemaphoreType.DMA((steps,))
        local = [
            pltpu.SMEM(block_order.shape, block_order.dtype),
            pltpu.VMEM(queries.shape, queries.dtype),
            pltpu.VMEM((CHUNKS, 2, piece, HD), key_rows.dtype),
        ]
        return pl.pallas_call(
            functools.partial(kernel, count),
            out_shape=jax.ShapeDtypeStruct(queries.shape, queries.dtype),
            in_specs=[pl.BlockSpec(memory_space=pl.ANY)] * 4,
            out_specs=pl.BlockSpec(memory_space=pltpu.VMEM),
            scratch_shapes=local + [slots] * 2 + [stats] * 3 + [sems] * 4 + [pltpu.SemaphoreType.DMA((2 * CHUNKS + 2,))],
            compiler_params=pltpu.CompilerParams(
                collective_id=0, has_side_effects=True
            ),
        )(block_order, queries, key_rows, value_rows)

    in_specs = (P("ctx", "head"), P("ctx", "head"), P("ctx", "head"), P())
    return jax.shard_map(body, mesh=mesh, in_specs=in_specs, out_specs=P("ctx", "head"), check_vma=False)
```

```python
import functools

import jax
import jax.numpy as jnp
from jax import lax
from jax.experimental import pallas as pl
from jax.experimental.pallas import tpu as pltpu
from jax.sharding import PartitionSpec as P

HD = 128
QH = 2
CHUNKS = 4
TILE = 1024
SCALE2 = 168.0 ** (-0.5) * 1.4426950408889634
LOW = -1e30


def ring_place(index, count):
    side = lax.rem(index, 2)
    level = lax.div(index, 2)
    return level * (1 - side) + (count - 1 - level) * side


def ring_index(place, count):
    side = lax.div(place, count // 2)
    level = place * (1 - side) + (count - 1 - place) * side
    return level * 2 + side


def lanes(column, width):
    return jnp.concatenate([column] * (width // HD), axis=1)


def dot_t(a, b):
    return lax.dot_general(a, b, (((1,), (1,)), ((), ())), preferred_element_type=jnp.float32)


def lane_sum(weights):
    total = weights[:, :HD]
    for start in range(HD, weights.shape[1], HD):
        total = total + weights[:, start : start + HD]
    return total


def kernel(
    count, order_hbm, q_hbm, k_hbm, v_hbm, out_ref,
    order_ref, q_ref, kv_ref, from_left, from_right, acc, peak, total,
    to_right_sem, to_left_sem, from_left_sem, from_right_sem, loaded,
):
    me = lax.axis_index("ctx")
    rows = q_ref.shape[0]
    band = min(TILE, rows)
    piece = rows // CHUNKS
    steps = CHUNKS * (count - 1) // 2
    place = ring_place(me, count)
    right = ring_index(lax.rem(place + 1, count), count)
    left = ring_index(lax.rem(place + count - 1, count), count)

    barrier = pltpu.get_barrier_semaphore()
    for neighbour in (left, right):
        pl.semaphore_signal(barrier, inc=1, device_id={"ctx": neighbour}, device_id_type=pl.DeviceIdType.MESH)
    def chunked(src, which):
        return [(src.at[pl.ds(c * piece, piece)], kv_ref.at[c, which]) for c in range(CHUNKS)]

    loads = [
        pltpu.make_async_copy(src, dst, loaded.at[which])
        for which, (src, dst) in enumerate(
            chunked(k_hbm, 0) + chunked(v_hbm, 1) + [(q_hbm, q_ref), (order_hbm, order_ref)]
        )
    ]
    for load in loads:
        load.start()
    for load in loads[:-2]:
        load.wait()
    pl.semaphore_wait(barrier, 2)

    def copy(j, rightward, src, slot):
        dst, send, recv, target = (
            (from_left, to_right_sem, from_left_sem, right)
            if rightward
            else (from_right, to_left_sem, from_right_sem, left)
        )
        return pltpu.make_async_remote_copy(
            src_ref=src.at[slot], dst_ref=dst.at[j], send_sem=send.at[j], recv_sem=recv.at[j],
            device_id={"ctx": target}, device_id_type=pl.DeviceIdType.MESH,
        )

    for j in range(CHUNKS):
        copy(j, True, kv_ref, j).start()
        copy(j, False, kv_ref, (j + CHUNKS // 2) % CHUNKS).start()
    for load in loads[-2:]:
        load.wait()

    for head in range(QH):
        cols = slice(head * HD, (head + 1) * HD)
        for tile in range(CHUNKS):
            here = slice(tile * piece, (tile + 1) * piece)
            width = (tile + 1) * piece
            scores = dot_t(q_ref[here, cols], kv_ref[: tile + 1, 0].reshape(width, HD))
            row_ids = lax.broadcasted_iota(jnp.int32, (piece, width), 0) + tile * piece
            column_ids = lax.broadcasted_iota(jnp.int32, (piece, width), 1)
            scores = jnp.where(column_ids <= row_ids, scores, LOW)
            top = jnp.broadcast_to(jnp.max(scores, axis=1, keepdims=True), (piece, HD))
            weights = jnp.exp2((scores - lanes(top, width)) * SCALE2)
            total[head, here, :] = lane_sum(weights)
            acc[head, here, :] = jnp.dot(
                weights.astype(jnp.bfloat16), kv_ref[: tile + 1, 1].reshape(width, HD), preferred_element_type=jnp.float32
            )
            peak[head, here, :] = top

    mine = order_ref[me]

    def arrive(j):
        copy(j, True, kv_ref, 0).wait_recv()
        copy(j, False, kv_ref, 0).wait_recv()

    def absorb(j, last):
        far = 1 + lax.div(j, CHUNKS)
        see_left = order_ref[ring_index(lax.rem(place + count - far, count), count)] < mine
        see_right = order_ref[ring_index(lax.rem(place + far, count), count)] < mine

        def tile_step(tile, carry):
            here = pl.ds(pl.multiple_of(tile * band, band), band)
            for head in range(QH):
                cols = slice(head * HD, (head + 1) * HD)
                q = q_ref[here, cols]
                first = dot_t(q, from_left[j, 0])
                second = dot_t(q, from_right[j, 0])
                old = peak[head, here, :]
                top_first = jnp.where(see_left, jnp.max(first, axis=1, keepdims=True), LOW)
                top_second = jnp.where(see_right, jnp.max(second, axis=1, keepdims=True), LOW)
                top = jnp.maximum(old, jnp.maximum(top_first, top_second))
                keep = jnp.exp2((old - top) * SCALE2)
                shift_first = jnp.where(see_left, top, -LOW)
                shift_second = jnp.where(see_right, top, -LOW)
                w_first = jnp.exp2((first - lanes(shift_first, piece)) * SCALE2)
                w_second = jnp.exp2((second - lanes(shift_second, piece)) * SCALE2)
                new_total = total[head, here, :] * keep + (lane_sum(w_first) + lane_sum(w_second))
                new_acc = acc[head, here, :] * keep + (
                    jnp.dot(w_first.astype(jnp.bfloat16), from_left[j, 1], preferred_element_type=jnp.float32)
                    + jnp.dot(w_second.astype(jnp.bfloat16), from_right[j, 1], preferred_element_type=jnp.float32)
                )
                if last:
                    inverse = 1.0 / jnp.sum(new_total, axis=1, keepdims=True)
                    out_ref[here, cols] = (new_acc * inverse).astype(out_ref.dtype)
                else:
                    peak[head, here, :] = top
                    total[head, here, :] = new_total
                    acc[head, here, :] = new_acc
            return carry

        lax.fori_loop(0, rows // band, tile_step, 0)

    def advance(j, carry):
        arrive(j)

        @pl.when(j + CHUNKS < steps)
        def _():
            copy(j + CHUNKS, True, from_left, j).start()
            copy(j + CHUNKS, False, from_right, j).start()

        absorb(j, False)
        return carry

    lax.fori_loop(0, steps - 1, advance, 0)
    arrive(steps - 1)
    absorb(steps - 1, True)

    def drain(j, carry):
        copy(j, True, kv_ref, 0).wait_send()
        copy(j, False, kv_ref, 0).wait_send()
        return carry

    lax.fori_loop(0, steps, drain, 0)


def solution(mesh):
    count = mesh.shape["ctx"]
    steps = CHUNKS * (count - 1) // 2

    def body(queries, key_rows, value_rows, block_order):
        rows = queries.shape[0]
        piece = rows // CHUNKS
        slots = pltpu.VMEM((steps, 2, piece, HD), jnp.bfloat16)
        stats = pltpu.VMEM((QH, rows, HD), jnp.float32)
        sems = pltpu.SemaphoreType.DMA((steps,))
        local = [
            pltpu.SMEM(block_order.shape, block_order.dtype),
            pltpu.VMEM(queries.shape, queries.dtype),
            pltpu.VMEM((CHUNKS, 2, piece, HD), key_rows.dtype),
        ]
        return pl.pallas_call(
            functools.partial(kernel, count),
            out_shape=jax.ShapeDtypeStruct(queries.shape, queries.dtype),
            in_specs=[pl.BlockSpec(memory_space=pltpu.HBM)] * 4,
            out_specs=pl.BlockSpec(memory_space=pltpu.VMEM),
            scratch_shapes=local + [slots] * 2 + [stats] * 3 + [sems] * 4 + [pltpu.SemaphoreType.DMA((2 * CHUNKS + 2,))],
            compiler_params=pltpu.CompilerParams(
                collective_id=0, has_side_effects=True, vmem_limit_bytes=48 * 1024 * 1024
            ),
        )(*(pltpu.with_memory_space_constraint(x, pltpu.HBM) for x in (block_order, queries, key_rows, value_rows)))

    in_specs = (P("ctx", "head"), P("ctx", "head"), P("ctx", "head"), P())
    return jax.shard_map(body, mesh=mesh, in_specs=in_specs, out_specs=P("ctx", "head"), check_vma=False)
```
